32 devices in a mesh: tm: 16 (over z, y, x), tile: 2 (over core).
Axes of the slice: x: 2, y: 2, z: 4, core: 2. Of those that a mesh axis runs over, the one named last changes fastest.
Arguments:
- latent: bfloat16 [64, 8, 160, 128], P('tm', 'tile'), may hold values from -6 to 6
- cot_forward: bfloat16 [64, 8, 160, 128], P('tm', 'tile'), may hold values from -6 to 6
- cot_reverse: bfloat16 [64, 8, 160, 128], P('tm', 'tile'), may hold values from -6 to 6
- spatial_weight: bfloat16 [3, 3, 128, 128], replicated, may hold values from -0.1875 to 0.1875
- temporal_weight: bfloat16 [3, 128, 128], replicated, may hold values from -0.3125 to 0.3125
Outputs:
- out_forward: bfloat16 [64, 8, 160, 128], P('tm', 'tile')
- out_reverse: bfloat16 [64, 8, 160, 128], P('tm', 'tile')
- grad_input: bfloat16 [64, 8, 160, 128], P('tm', 'tile')
- grad_spatial: float32 [3, 3, 128, 128], replicated
- grad_temporal: float32 [3, 128, 128], replicated
The draws below stay inside these ranges and needn't reach their ends.
All inputs are finite; a program needn't handle non-finite values.
Results may differ from the reference program's by a relative error of at most 0.0032.
Values may be sent and summed in bfloat16 or wider, within the bound.
A program may use at most 64 MiB of HBM per device.

```python
import math
import jax
import jax.numpy as jnp
from jax import lax

C = 128
W = 160
FRAMES = 64
ROWS = 8


def levels(key, extent, pieces, least, largest):
    factor_of, own = 1.0, jax.random.fold_in(key, 6)
    for axis_at, blocks in pieces:
        steps = jnp.exp(jax.random.uniform(jax.random.fold_in(own, axis_at), (blocks,), jnp.float32, least / len(pieces), largest / len(pieces)))
        factor_of = factor_of * jnp.repeat(steps, extent[axis_at] // blocks).reshape([-1 if axis == axis_at else 1 for axis in range(len(extent))])
    return factor_of


def noise(stream_key, extent, spread, reach, pieces=(), kind=jnp.bfloat16):
    drawn = jax.random.normal(stream_key, extent, jnp.float32) * spread
    if len(pieces) > 0:
        drawn = levels(stream_key, extent, pieces, -0.22, 0.18) * drawn
    return jnp.clip(drawn, min=-reach, max=reach).astype(kind)


def setup_inputs(seed: int = 0) -> dict:
    splits = jax.random.split(jax.random.key(seed), 6)
    latent = noise(splits[0], (FRAMES, ROWS, W, C), 1.0, 6.0, ((0, 16), (1, 2)))
    cot_forward = noise(splits[1], (FRAMES, ROWS, W, C), 1.0, 6.0, ((0, 16), (1, 2)))
    cot_reverse = noise(splits[2], (FRAMES, ROWS, W, C), 1.0, 6.0, ((0, 16), (1, 2)))
    spatial_weight = noise(splits[3], (3, 3, C, C), (9 * C) ** -0.5, 0.1875)
    temporal_weight = noise(splits[4], (3, C, C), (3 * C) ** -0.5, 0.3125)
    return {"latent": latent, "cot_forward": cot_forward, "cot_reverse": cot_reverse, "spatial_weight": spatial_weight, "temporal_weight": temporal_weight}


def flat(values):
    return values.reshape(-1, values.shape[-1])

def shift_frames(values, lag_steps):
    if lag_steps > 0:
        return jnp.concatenate([jnp.zeros_like(values[:lag_steps]), values[:-lag_steps]], axis=0)
    if lag_steps < 0:
        return jnp.concatenate([values[-lag_steps:], jnp.zeros_like(values[:-lag_steps])], axis=0)
    return values

def contract_rows(left, right):
    return lax.dot_general(left, right, (((0,), (0,)), ((), ())), preferred_element_type=jnp.float32)

def reference(latent, cot_forward, cot_reverse, spatial_weight, temporal_weight):
    frame_count, height, width_cells, channels = latent.shape
    padded = jnp.pad(latent, ((0, 0), (1, 1), (1, 1), (0, 0)))
    pre_act = jnp.zeros((frame_count * height * width_cells, channels), jnp.float32)
    for row_step in range(3):
        for col_step in range(3):
            window = flat(padded[:, row_step:row_step + height, col_step:col_step + width_cells, :])
            pre_act = pre_act + jnp.dot(window, spatial_weight[row_step, col_step], preferred_element_type=jnp.float32)
    act = jax.nn.silu(pre_act).astype(jnp.bfloat16).reshape(latent.shape)

    def causal_out(source_latent, source_act):
        total = flat(source_latent).astype(jnp.float32)
        for lag_steps in range(3):
            total = total + jnp.dot(flat(shift_frames(source_act, lag_steps)), temporal_weight[lag_steps], preferred_element_type=jnp.float32)
        return total.astype(jnp.bfloat16).reshape(latent.shape)
    out_forward = causal_out(latent, act)
    out_reverse = causal_out(latent[::-1], act[::-1])[::-1]
    grad_act = jnp.zeros((frame_count * height * width_cells, channels), jnp.float32)
    grad_temp = []
    for lag_steps in range(3):
        weight_back = jnp.transpose(temporal_weight[lag_steps])
        grad_act = grad_act + jnp.dot(flat(shift_frames(cot_forward, -lag_steps)), weight_back, preferred_element_type=jnp.float32)
        grad_act = grad_act + jnp.dot(flat(shift_frames(cot_reverse, lag_steps)), weight_back, preferred_element_type=jnp.float32)
        term = contract_rows(flat(shift_frames(act, lag_steps)), flat(cot_forward))
        term = term + contract_rows(flat(shift_frames(act, -lag_steps)), flat(cot_reverse))
        grad_temp.append(term)
    sigmoid_pre = jax.nn.sigmoid(pre_act)
    grad_pre = (grad_act * sigmoid_pre * (1.0 + pre_act * (1.0 - sigmoid_pre))).astype(jnp.bfloat16)
    grad_padded = jnp.pad(grad_pre.reshape(latent.shape), ((0, 0), (1, 1), (1, 1), (0, 0)))
    total_in = flat(cot_forward).astype(jnp.float32) + flat(cot_reverse).astype(jnp.float32)
    grad_space = []
    for row_step in range(3):
        for col_step in range(3):
            window = flat(grad_padded[:, 2 - row_step:2 - row_step + height, 2 - col_step:2 - col_step + width_cells, :])
            total_in = total_in + jnp.dot(window, jnp.transpose(spatial_weight[row_step, col_step]), preferred_element_type=jnp.float32)
            source = flat(padded[:, row_step:row_step + height, col_step:col_step + width_cells, :])
            grad_space.append(contract_rows(source, grad_pre))
    grad_input = total_in.astype(jnp.bfloat16).reshape(latent.shape)
    grad_scale = 1.0 / math.sqrt(frame_count * height * width_cells)
    grad_spatial = jnp.stack(grad_space).reshape(3, 3, channels, channels) * grad_scale
    grad_temporal = jnp.stack(grad_temp) * grad_scale
    return (out_forward, out_reverse, grad_input, grad_spatial, grad_temporal)
```

```python
import functools
import math

import jax
import jax.numpy as jnp
from jax import lax
from jax.experimental import pallas as pl
from jax.experimental.pallas import tpu as pltpu
from jax.sharding import PartitionSpec as P


def extended_2(cells, sides, width):
    for axis, dim in sides:
        count = lax.axis_size(axis)
        ends = count - 1
        head = lax.slice_in_dim(cells, 0, width, axis=dim)
        tail = lax.slice_in_dim(cells, cells.shape[dim] - width, cells.shape[dim], axis=dim)
        cells = jnp.concatenate(
            [
                lax.ppermute(tail, axis, [(i, (i + 1) % count) for i in range(ends)]),
                cells,
                lax.ppermute(head, axis, [((i + 1) % count, i) for i in range(ends)]),
            ],
            axis=dim,
        )
    return cells


def shifted(value, axis, steps):
    count = lax.axis_size(axis)
    initial, last = (max(0, -steps), min(count, count - steps))
    return lax.ppermute(value, axis, [(source, source + steps) for source in range(initial, last)])


def spatial_rows(padded, height, width_cells, flipped):
    pieces = []
    for row_step in range(3):
        for col_step in range(3):
            row_from = 2 - row_step if flipped else row_step
            col_from = 2 - col_step if flipped else col_step
            pieces.append(
                padded[:, row_from : row_from + height, col_from : col_from + width_cells, :]
            )
    joined = jnp.concatenate(pieces, axis=3)
    return joined.reshape(-1, joined.shape[3])


def widen(values):
    return jnp.pad(values, ((0, 0), (0, 0), (1, 1), (0, 0)))


def temporal_rows(extended, offsets, frame_count):
    joined = jnp.concatenate(
        [extended[offset : offset + frame_count] for offset in offsets], axis=2
    )
    return joined.reshape(-1, joined.shape[2])


def contract_rows(left, right):
    return lax.dot_general(
        left, right, (((0,), (0,)), ((), ())), preferred_element_type=jnp.float32
    )


MESH = pl.DeviceIdType.MESH


def sum_kernel(tiles, shards, scale, x_ref, o_ref, pair_in, mid, shard_in, send_sem, recv_sem):
    tile, shard = lax.axis_index("tile"), lax.axis_index("tm")
    rows = x_ref.shape[0]
    half = rows // tiles
    chunk = half // shards

    def tile_peer(step):
        return lax.rem(tile + step, tiles)

    def shard_peer(step):
        return lax.rem(shard + step, shards)

    def at(start, size):
        return pl.ds(pl.multiple_of(start, 8), size)

    def each(count, act):
        def step(index, carry):
            act(index)
            return carry

        lax.fori_loop(1, count, step, 0)

    def settle(phase, ref):
        pltpu.make_async_copy(ref, ref, send_sem.at[phase]).wait()
        pltpu.make_async_copy(ref, ref, recv_sem.at[phase]).wait()

    def send(src, dst, phase, peer):
        pltpu.make_async_remote_copy(
            src_ref=src,
            dst_ref=dst,
            send_sem=send_sem.at[phase],
            recv_sem=recv_sem.at[phase],
            device_id=peer,
            device_id_type=MESH,
        ).start()

    barrier = pltpu.get_barrier_semaphore()
    each(
        tiles,
        lambda step: pl.semaphore_signal(
            barrier, inc=1, device_id={"tile": tile_peer(step)}, device_id_type=MESH
        ),
    )
    each(
        shards,
        lambda step: pl.semaphore_signal(
            barrier, inc=1, device_id={"tm": shard_peer(step)}, device_id_type=MESH
        ),
    )
    pl.semaphore_wait(barrier, tiles + shards - 2)

    each(
        tiles,
        lambda step: send(
            x_ref.at[at(tile_peer(step) * half, half)],
            pair_in.at[step - 1],
            0,
            {"tile": tile_peer(step)},
        ),
    )
    settle(0, pair_in)
    total = x_ref[at(tile * half, half), :]
    for index in range(tiles - 1):
        total = total + pair_in[index]
    mid[...] = total
    each(
        shards,
        lambda step: send(
            mid.at[at(shard_peer(step) * chunk, chunk)],
            shard_in.at[step - 1],
            1,
            {"tm": shard_peer(step)},
        ),
    )
    settle(1, shard_in)
    part = lax.fori_loop(
        0,
        shards - 1,
        lambda index, value: value + shard_in[index],
        mid[at(shard * chunk, chunk), :],
    )
    own = at(tile * half + shard * chunk, chunk)
    o_ref[own, :] = part * scale
    each(shards, lambda step: send(o_ref.at[own], o_ref.at[own], 2, {"tm": shard_peer(step)}))
    settle(2, o_ref.at[pl.ds(0, (shards - 1) * chunk)])
    mine = at(tile * half, half)
    each(tiles, lambda step: send(o_ref.at[mine], o_ref.at[mine], 3, {"tile": tile_peer(step)}))
    settle(3, o_ref.at[pl.ds(0, (tiles - 1) * half)])


def summed(values, scale):
    tiles, shards = lax.axis_size("tile"), lax.axis_size("tm")
    rows, channels = values.shape
    unit = 8 * tiles * shards
    padded = -(-rows // unit) * unit
    if padded > rows:
        values = jnp.pad(values, ((0, padded - rows), (0, 0)))
    half = padded // tiles
    chunk = half // shards
    out = pl.pallas_call(
        functools.partial(sum_kernel, tiles, shards, scale),
        out_shape=jax.ShapeDtypeStruct(values.shape, jnp.float32),
        in_specs=[pl.BlockSpec(memory_space=pltpu.VMEM)],
        out_specs=pl.BlockSpec(memory_space=pltpu.VMEM),
        scratch_shapes=[
            pltpu.VMEM((tiles - 1, half, channels), jnp.float32),
            pltpu.VMEM((half, channels), jnp.float32),
            pltpu.VMEM((shards - 1, chunk, channels), jnp.float32),
            pltpu.SemaphoreType.DMA((4,)),
            pltpu.SemaphoreType.DMA((4,)),
        ],
        compiler_params=pltpu.CompilerParams(collective_id=0, has_side_effects=True),
    )(values)
    return out[:rows]


def body(latent, cot_forward, cot_reverse, spatial_weight, temporal_weight):
    frame_count, height, width_cells, channels = latent.shape
    plane_cells = height * width_cells
    spatial_flat = spatial_weight.reshape(9 * channels, channels)
    flipped_flat = jnp.transpose(spatial_weight, (0, 1, 3, 2)).reshape(9 * channels, channels)
    forward_flat = temporal_weight.reshape(3 * channels, channels)
    backward_flat = jnp.transpose(temporal_weight, (0, 2, 1)).reshape(3 * channels, channels)
    latent_flat = latent.reshape(-1, channels)
    fwd_cot = cot_forward.reshape(frame_count, plane_cells, channels)
    rev_cot = cot_reverse.reshape(frame_count, plane_cells, channels)
    rimmed = extended_2(latent, (("tile", 1),), 1)
    patches = spatial_rows(widen(rimmed), height, width_cells, False)
    pre_act = jnp.dot(patches, spatial_flat, preferred_element_type=jnp.float32)
    act_frames = (
        jax.nn.silu(pre_act).astype(jnp.bfloat16).reshape(frame_count, plane_cells, channels)
    )
    rimmed_act = extended_2(act_frames, (("tm", 0),), 2)
    following = shifted(fwd_cot[:2], "tm", -1)
    earlier = shifted(rev_cot[-2:], "tm", 1)
    causal = temporal_rows(rimmed_act, (2, 1, 0), frame_count)
    anticausal = temporal_rows(rimmed_act, (2, 3, 4), frame_count)
    residual_in = latent_flat.astype(jnp.float32)
    out_forward = (
        (residual_in + jnp.dot(causal, forward_flat, preferred_element_type=jnp.float32))
        .astype(jnp.bfloat16)
        .reshape(latent.shape)
    )
    out_reverse = (
        (residual_in + jnp.dot(anticausal, forward_flat, preferred_element_type=jnp.float32))
        .astype(jnp.bfloat16)
        .reshape(latent.shape)
    )
    ahead_rows = temporal_rows(
        jnp.concatenate([fwd_cot, following], axis=0), (0, 1, 2), frame_count
    )
    behind = temporal_rows(jnp.concatenate([earlier, rev_cot], axis=0), (2, 1, 0), frame_count)
    grad_act = jnp.dot(ahead_rows, backward_flat, preferred_element_type=jnp.float32)
    grad_act = grad_act + jnp.dot(behind, backward_flat, preferred_element_type=jnp.float32)
    grad_temp = contract_rows(causal, cot_forward.reshape(-1, channels))
    grad_temp = grad_temp + contract_rows(anticausal, cot_reverse.reshape(-1, channels))
    sigmoid_pre = jax.nn.sigmoid(pre_act)
    grad_pre = (grad_act * sigmoid_pre * (1.0 + pre_act * (1.0 - sigmoid_pre))).astype(jnp.bfloat16)
    grad_rim = extended_2(grad_pre.reshape(latent.shape), (("tile", 1),), 1)
    grad_patches = spatial_rows(widen(grad_rim), height, width_cells, True)
    total_in = cot_forward.reshape(-1, channels).astype(jnp.float32) + cot_reverse.reshape(
        -1, channels
    ).astype(jnp.float32)
    total_in = total_in + jnp.dot(grad_patches, flipped_flat, preferred_element_type=jnp.float32)
    grad_input = total_in.astype(jnp.bfloat16).reshape(latent.shape)
    grad_space = contract_rows(patches, grad_pre)
    positions = frame_count * height * width_cells * lax.axis_size("tm") * lax.axis_size("tile")
    grad_scale = 1.0 / math.sqrt(positions)
    grads = summed(jnp.concatenate([grad_space, grad_temp], axis=0), grad_scale)
    grad_spatial = grads[: 9 * channels].reshape(3, 3, channels, channels)
    grad_temporal = grads[9 * channels :].reshape(3, channels, channels)
    return (out_forward, out_reverse, grad_input, grad_spatial, grad_temporal)


def solution(mesh):
    placed = (
        P("tm", "tile", None, None),
        P("tm", "tile", None, None),
        P("tm", "tile", None, None),
        P(),
        P(),
    )
    return jax.shard_map(
        body,
        mesh=mesh,
        in_specs=placed,
        out_specs=(
            P("tm", "tile", None, None),
            P("tm", "tile", None, None),
            P("tm", "tile", None, None),
            P(),
            P(),
        ),
        check_vma=False,
    )
```

```python
import functools
import math

import jax
import jax.numpy as jnp
from jax import lax
from jax.experimental import pallas as pl
from jax.experimental.pallas import tpu as pltpu
from jax.sharding import PartitionSpec as P

MESH = pl.DeviceIdType.MESH


def at(start, size):
    return pl.ds(pl.multiple_of(start, 8), size)


def each(count, act):
    def step(index, carry):
        act(index)
        return carry

    lax.fori_loop(1, count, step, 0)


def frames(first, last, act):
    def step(index, carry):
        act(index)
        return carry

    lax.fori_loop(first, last, step, 0)


def columns(rows, width, channels):
    place = lax.broadcasted_iota(jnp.int32, (rows // width, width, channels), 1)
    return place.reshape(rows, channels)


def before(value, place):
    return jnp.where(place == 0, 0.0, pltpu.roll(value, 1, 0))


def after(value, place, width):
    return jnp.where(place == width - 1, 0.0, pltpu.roll(value, value.shape[0] - 1, 0))


def spread(value, place, width):
    kind = jnp.bfloat16
    return jnp.concatenate(
        [after(value, place, width).astype(kind), value.astype(kind), before(value, place).astype(kind)],
        axis=1,
    )


def flat(value):
    return value.reshape(-1, value.shape[-1])


def across(left, right):
    return lax.dot_general(
        left, right, (((1,), (1,)), ((), ())), preferred_element_type=jnp.float32
    )


def contract(left, right):
    return lax.dot_general(
        left, right, (((0,), (0,)), ((), ())), preferred_element_type=jnp.float32
    )


def kernel(
    tiles,
    shards,
    scale,
    latent_ref,
    fwd_ref,
    rev_ref,
    space_ref,
    time_ref,
    out_f_ref,
    out_r_ref,
    grad_in_ref,
    grad_s_ref,
    grad_t_ref,
    cells,
    cot_f,
    cot_r,
    acts,
    pre,
    wide,
    rim_out,
    rim_in,
    space_fwd,
    space_back,
    time_back,
    sums,
    pair_in,
    mid,
    shard_in,
    total,
    load_sem,
    send_sem,
    recv_sem,
):
    tile, shard = lax.axis_index("tile"), lax.axis_index("tm")
    count, height, width, channels = latent_ref.shape
    plane = height * width
    taps = 3

    def tile_peer(step):
        return {"tile": lax.rem(tile + step, tiles)}

    def shard_peer(step):
        return {"tm": lax.rem(shard + step, shards)}

    barrier = pltpu.get_barrier_semaphore()

    def greet(peer):
        pl.semaphore_signal(barrier, inc=1, device_id=peer, device_id_type=MESH)

    each(tiles, lambda step: greet(tile_peer(step)))
    each(shards, lambda step: greet(shard_peer(step)))

    loads = [
        pltpu.make_async_copy(latent_ref, cells.at[:, pl.ds(1, height)], load_sem.at[0]),
        pltpu.make_async_copy(fwd_ref, cot_f.at[pl.ds(0, count)], load_sem.at[1]),
        pltpu.make_async_copy(rev_ref, cot_r.at[pl.ds(2, count)], load_sem.at[2]),
    ]
    for load in loads:
        load.start()

    has_next_tile, has_last_tile = tile < tiles - 1, tile > 0
    has_next_shard, has_last_shard = shard < shards - 1, shard > 0

    def remote(src, dst, index, peer):
        return pltpu.make_async_remote_copy(
            src_ref=src,
            dst_ref=dst,
            send_sem=send_sem.at[index],
            recv_sem=recv_sem.at[index],
            device_id=peer,
            device_id_type=MESH,
        )

    next_tile, last_tile = tile_peer(1), tile_peer(tiles - 1)
    next_shard, last_shard = shard_peer(1), shard_peer(shards - 1)
    moves = [
        (latent_ref.at[:, height - 1], cells.at[:, 0], next_tile, has_next_tile, has_last_tile),
        (latent_ref.at[:, 0], cells.at[:, height + 1], last_tile, has_last_tile, has_next_tile),
        (
            fwd_ref.at[pl.ds(0, 2)],
            cot_f.at[pl.ds(count, 2)],
            last_shard,
            has_last_shard,
            has_next_shard,
        ),
        (
            rev_ref.at[pl.ds(count - 2, 2)],
            cot_r.at[pl.ds(0, 2)],
            next_shard,
            has_next_shard,
            has_last_shard,
        ),
        (
            acts.at[pl.ds(count, 2)],
            acts.at[pl.ds(0, 2)],
            next_shard,
            has_next_shard,
            has_last_shard,
        ),
        (
            acts.at[pl.ds(2, 2)],
            acts.at[pl.ds(count + 2, 2)],
            last_shard,
            has_last_shard,
            has_next_shard,
        ),
        (rim_out.at[1], rim_in.at[0], next_tile, has_next_tile, has_last_tile),
        (rim_out.at[0], rim_in.at[1], last_tile, has_last_tile, has_next_tile),
    ]
    copies = [remote(src, dst, index, peer) for index, (src, dst, peer, _, _) in enumerate(moves)]

    def launch(index):
        pl.when(moves[index][3])(copies[index].start)

    def arrive(index):
        pl.when(moves[index][4])(copies[index].wait_recv)

    def leave(index):
        pl.when(moves[index][3])(copies[index].wait_send)

    for index in range(8):
        if index < 6:
            target = moves[index][1]

            @pl.when(jnp.logical_not(moves[index][4]))
            def _(target=target):
                target[...] = jnp.zeros(target.shape, target.dtype)

        else:
            target = rim_in.at[index - 6]

            @pl.when(jnp.logical_not(moves[index][4]))
            def _(target=target):
                target[...] = jnp.zeros(target.shape, target.dtype)

    sums[...] = jnp.zeros_like(sums)
    for row in range(taps):
        time_back[:, row * channels : (row + 1) * channels] = time_ref[
            row * channels : (row + 1) * channels, :
        ]
        time_back[:, (taps + row) * channels : (taps + row + 1) * channels] = time_ref[
            row * channels : (row + 1) * channels, :
        ]
        for col in range(taps):
            index = row * taps + col
            weight = space_ref[index * channels : (index + 1) * channels, :]
            space_fwd[
                row * channels : (row + 1) * channels, col * channels : (col + 1) * channels
            ] = weight
            space_back[:, index * channels : (index + 1) * channels] = weight

    pl.semaphore_wait(barrier, tiles + shards - 2)
    for index in range(4):
        launch(index)
    place = columns(plane, width, channels)

    def window(frame):
        return jnp.concatenate(
            [flat(cells[frame, pl.ds(row, height)]) for row in range(taps)], axis=1
        )

    loads[0].wait()
    arrive(0)
    arrive(1)

    def convolve(frame):
        parts = jnp.dot(window(frame), space_fwd[...], preferred_element_type=jnp.float32)
        value = (
            before(parts[:, :channels], place)
            + parts[:, channels : 2 * channels]
            + after(parts[:, 2 * channels :], place, width)
        )
        pre[frame] = value
        act = value / (1.0 + jnp.exp(-value))
        acts[frame + 2] = act.astype(jnp.bfloat16).reshape(height, width, channels)

    frames(0, count, convolve)
    launch(4)
    launch(5)

    loads[1].wait()
    loads[2].wait()
    arrive(2)
    arrive(3)

    def backward(frame):
        joined = jnp.concatenate(
            [flat(cot_f[frame + lag]) for lag in range(taps)]
            + [flat(cot_r[frame + 2 - lag]) for lag in range(taps)],
            axis=1,
        )
        grad_act = across(joined, time_back[...])
        value = pre[frame]
        gate = 1.0 / (1.0 + jnp.exp(-value))
        grad = grad_act * gate * (1.0 + value * (1.0 - gate))
        grad = grad.astype(jnp.bfloat16).astype(jnp.float32)
        shifted = spread(grad, place, width)
        wide[frame, pl.ds(1, height)] = shifted.reshape(height, width, taps * channels)
        rounded = grad.astype(jnp.bfloat16)
        rim_out[0, frame] = rounded[:width]
        rim_out[1, frame] = rounded[plane - width :]
        lags = contract(flat(acts[frame + 2]), joined)
        for lag in range(taps):
            row = (taps * taps + lag) * channels
            sums[row : row + channels, :] += (
                lags[:, lag * channels : (lag + 1) * channels]
                + lags[:, (taps + lag) * channels : (taps + lag + 1) * channels]
            )
        part = contract(window(frame), shifted)
        for row in range(taps):
            for col in range(taps):
                start = (row * taps + col) * channels
                sums[start : start + channels, :] += part[
                    row * channels : (row + 1) * channels, col * channels : (col + 1) * channels
                ]

    frames(0, count, backward)
    launch(6)
    launch(7)

    half = sums.shape[0] // tiles
    chunk = half // shards

    def settle(phase, ref):
        pltpu.make_async_copy(ref, ref, send_sem.at[phase]).wait()
        pltpu.make_async_copy(ref, ref, recv_sem.at[phase]).wait()

    def rows_to(step):
        return lax.rem(tile + step, tiles) * half

    each(
        tiles,
        lambda step: remote(
            sums.at[at(rows_to(step), half)], pair_in.at[step - 1], 8, tile_peer(step)
        ).start(),
    )

    def outputs(frame):
        base = flat(cells[frame, pl.ds(1, height)]).astype(jnp.float32)
        causal = jnp.concatenate([flat(acts[frame + 2 - lag]) for lag in range(taps)], axis=1)
        anticausal = jnp.concatenate([flat(acts[frame + 2 + lag]) for lag in range(taps)], axis=1)
        for joined, ref in ((causal, out_f_ref), (anticausal, out_r_ref)):
            value = base + jnp.dot(joined, time_ref[...], preferred_element_type=jnp.float32)
            ref[frame] = value.astype(jnp.bfloat16).reshape(height, width, channels)

    def input_grads(frame):
        joined = jnp.concatenate(
            [flat(wide[frame, pl.ds(2 - row, height)]) for row in range(taps)], axis=1
        )
        value = flat(cot_f[frame]).astype(jnp.float32) + flat(cot_r[frame + 2]).astype(jnp.float32)
        value = value + across(joined, space_back[...])
        grad_in_ref[frame] = value.astype(jnp.bfloat16).reshape(height, width, channels)

    settle(8, pair_in)
    own_half = sums[at(tile * half, half), :]
    for index in range(tiles - 1):
        own_half = own_half + pair_in[index]
    mid[...] = own_half
    each(
        shards,
        lambda step: remote(
            mid.at[at(lax.rem(shard + step, shards) * chunk, chunk)],
            shard_in.at[step - 1],
            9,
            shard_peer(step),
        ).start(),
    )
    arrive(4)
    arrive(5)
    frames(0, count, outputs)
    settle(9, shard_in)
    part = lax.fori_loop(
        0,
        shards - 1,
        lambda index, value: value + shard_in[index],
        mid[at(shard * chunk, chunk), :],
    )
    own = at(tile * half + shard * chunk, chunk)
    total[own, :] = part * scale
    each(
        shards,
        lambda step: remote(total.at[own], total.at[own], 10, shard_peer(step)).start(),
    )
    arrive(6)
    arrive(7)
    edge = columns(count * width, width, channels)
    for side, row in ((0, 0), (1, height + 1)):
        rim = spread(flat(rim_in[side]).astype(jnp.float32), edge, width)
        wide[:, row] = rim.reshape(count, width, taps * channels)
    frames(0, count, input_grads)
    settle(10, total.at[pl.ds(0, (shards - 1) * chunk)])
    mine = at(tile * half, half)
    each(
        tiles,
        lambda step: remote(total.at[mine], total.at[mine], 11, tile_peer(step)).start(),
    )
    for index in range(8):
        leave(index)
    settle(11, total.at[pl.ds(0, (tiles - 1) * half)])
    split = taps * taps * channels
    grad_s_ref[...] = total[:split, :]
    grad_t_ref[...] = total[split : split + taps * channels, :]


def body(latent, cot_forward, cot_reverse, spatial_weight, temporal_weight):
    tiles, shards = lax.axis_size("tile"), lax.axis_size("tm")
    count, height, width, channels = latent.shape
    positions = count * height * width * shards * tiles
    scale = 1.0 / math.sqrt(positions)
    rows = 12 * channels
    unit = 8 * tiles * shards
    padded = -(-rows // unit) * unit
    half = padded // tiles
    chunk = half // shards
    kind = jnp.bfloat16
    vmem = pl.BlockSpec(memory_space=pltpu.VMEM)
    hbm = pl.BlockSpec(memory_space=pl.ANY)
    out_f, out_r, grad_in, grad_s, grad_t = pl.pallas_call(
        functools.partial(kernel, tiles, shards, scale),
        out_shape=(
            jax.ShapeDtypeStruct(latent.shape, kind),
            jax.ShapeDtypeStruct(latent.shape, kind),
            jax.ShapeDtypeStruct(latent.shape, kind),
            jax.ShapeDtypeStruct((9 * channels, channels), jnp.float32),
            jax.ShapeDtypeStruct((3 * channels, channels), jnp.float32),
        ),
        in_specs=[hbm, hbm, hbm, vmem, vmem],
        out_specs=(vmem, vmem, vmem, vmem, vmem),
        scratch_shapes=[
            pltpu.VMEM((count, height + 2, width, channels), kind),
            pltpu.VMEM((count + 2, height, width, channels), kind),
            pltpu.VMEM((count + 2, height, width, channels), kind),
            pltpu.VMEM((count + 4, height, width, channels), kind),
            pltpu.VMEM((count, height * width, channels), jnp.float32),
            pltpu.VMEM((count, height + 2, width, 3 * channels), kind),
            pltpu.VMEM((2, count, width, channels), kind),
            pltpu.VMEM((2, count, width, channels), kind),
            pltpu.VMEM((3 * channels, 3 * channels), kind),
            pltpu.VMEM((channels, 9 * channels), kind),
            pltpu.VMEM((channels, 6 * channels), kind),
            pltpu.VMEM((padded, channels), jnp.float32),
            pltpu.VMEM((tiles - 1, half, channels), jnp.float32),
            pltpu.VMEM((half, channels), jnp.float32),
            pltpu.VMEM((shards - 1, chunk, channels), jnp.float32),
            pltpu.VMEM((padded, channels), jnp.float32),
            pltpu.SemaphoreType.DMA((3,)),
            pltpu.SemaphoreType.DMA((12,)),
            pltpu.SemaphoreType.DMA((12,)),
        ],
        compiler_params=pltpu.CompilerParams(collective_id=0, has_side_effects=True),
    )(
        latent,
        cot_forward,
        cot_reverse,
        spatial_weight.reshape(9 * channels, channels),
        temporal_weight.reshape(3 * channels, channels),
    )
    return (
        out_f,
        out_r,
        grad_in,
        grad_s.reshape(spatial_weight.shape),
        grad_t.reshape(temporal_weight.shape),
    )


def solution(mesh):
    placed = (
        P("tm", "tile", None, None),
        P("tm", "tile", None, None),
        P("tm", "tile", None, None),
        P(),
        P(),
    )
    return jax.shard_map(
        body,
        mesh=mesh,
        in_specs=placed,
        out_specs=(
            P("tm", "tile", None, None),
            P("tm", "tile", None, None),
            P("tm", "tile", None, None),
            P(),
            P(),
        ),
        check_vma=False,
    )
```

```python
import functools
import math

import jax
import jax.numpy as jnp
from jax import lax
from jax.experimental import pallas as pl
from jax.experimental.pallas import tpu as pltpu
from jax.sharding import PartitionSpec as P

MESH = pl.DeviceIdType.MESH
PAIR_WIRE = jnp.bfloat16
PART_WIRE = jnp.bfloat16
SUM_WIRE = jnp.bfloat16


def at(start, size):
    return pl.ds(pl.multiple_of(start, 16), size)


def each(count, act):
    def step(index, carry):
        act(index)
        return carry

    lax.fori_loop(1, count, step, 0)


def frames(first, last, act):
    def step(index, carry):
        act(index)
        return carry

    lax.fori_loop(first, last, step, 0)


def columns(rows, width, channels):
    place = lax.broadcasted_iota(jnp.int32, (rows // width, width, channels), 1)
    return place.reshape(rows, channels)


def before(value, place):
    return jnp.where(place == 0, 0.0, pltpu.roll(value, 1, 0))


def after(value, place, width):
    return jnp.where(place == width - 1, 0.0, pltpu.roll(value, value.shape[0] - 1, 0))


def spread(value, place, width):
    kind = jnp.bfloat16
    return jnp.concatenate(
        [after(value, place, width).astype(kind), value.astype(kind), before(value, place).astype(kind)],
        axis=1,
    )


def flat(value):
    return value.reshape(-1, value.shape[-1])


def across(left, right):
    return lax.dot_general(
        left, right, (((1,), (1,)), ((), ())), preferred_element_type=jnp.float32
    )


def contract(left, right):
    return lax.dot_general(
        left, right, (((0,), (0,)), ((), ())), preferred_element_type=jnp.float32
    )


def kernel(
    tiles,
    shards,
    scale,
    latent_ref,
    fwd_ref,
    rev_ref,
    space_ref,
    time_ref,
    out_f_ref,
    out_r_ref,
    grad_in_ref,
    grad_s_ref,
    grad_t_ref,
    cells,
    cot_f,
    cot_r,
    acts,
    pre,
    wide,
    rim_out,
    rim_in,
    space_fwd,
    space_back,
    time_back,
    sums,
    pair_out,
    pair_in,
    mid,
    mid_out,
    shard_in,
    total,
    out_f,
    out_r,
    grad_in,
    grad_s,
    grad_t,
    load_sem,
    store_sem,
    send_sem,
    recv_sem,
):
    tile, shard = lax.axis_index("tile"), lax.axis_index("tm")
    count, height, width, channels = latent_ref.shape
    plane = height * width
    taps = 3

    def tile_peer(step):
        return {"tile": lax.rem(tile + step, tiles)}

    def shard_peer(step):
        return {"tm": lax.rem(shard + step, shards)}

    barrier = pltpu.get_barrier_semaphore()

    def greet(peer):
        pl.semaphore_signal(barrier, inc=1, device_id=peer, device_id_type=MESH)

    each(tiles, lambda step: greet(tile_peer(step)))
    each(shards, lambda step: greet(shard_peer(step)))

    loads = [
        pltpu.make_async_copy(latent_ref, cells.at[:, pl.ds(1, height)], load_sem.at[0]),
        pltpu.make_async_copy(fwd_ref, cot_f.at[pl.ds(0, count)], load_sem.at[1]),
        pltpu.make_async_copy(rev_ref, cot_r.at[pl.ds(2, count)], load_sem.at[2]),
    ]
    for load in loads:
        load.start()

    has_next_tile, has_last_tile = tile < tiles - 1, tile > 0
    has_next_shard, has_last_shard = shard < shards - 1, shard > 0

    def remote(src, dst, index, peer):
        return pltpu.make_async_remote_copy(
            src_ref=src,
            dst_ref=dst,
            send_sem=send_sem.at[index],
            recv_sem=recv_sem.at[index],
            device_id=peer,
            device_id_type=MESH,
        )

    next_tile, last_tile = tile_peer(1), tile_peer(tiles - 1)
    next_shard, last_shard = shard_peer(1), shard_peer(shards - 1)
    moves = [
        (latent_ref.at[:, height - 1], cells.at[:, 0], next_tile, has_next_tile, has_last_tile),
        (latent_ref.at[:, 0], cells.at[:, height + 1], last_tile, has_last_tile, has_next_tile),
        (
            fwd_ref.at[pl.ds(0, 2)],
            cot_f.at[pl.ds(count, 2)],
            last_shard,
            has_last_shard,
            has_next_shard,
        ),
        (
            rev_ref.at[pl.ds(count - 2, 2)],
            cot_r.at[pl.ds(0, 2)],
            next_shard,
            has_next_shard,
            has_last_shard,
        ),
        (
            acts.at[pl.ds(count, 2)],
            acts.at[pl.ds(0, 2)],
            next_shard,
            has_next_shard,
            has_last_shard,
        ),
        (
            acts.at[pl.ds(2, 2)],
            acts.at[pl.ds(count + 2, 2)],
            last_shard,
            has_last_shard,
            has_next_shard,
        ),
        (rim_out.at[1], rim_in.at[0], next_tile, has_next_tile, has_last_tile),
        (rim_out.at[0], rim_in.at[1], last_tile, has_last_tile, has_next_tile),
    ]
    copies = [remote(src, dst, index, peer) for index, (src, dst, peer, _, _) in enumerate(moves)]

    def launch(index):
        pl.when(moves[index][3])(copies[index].start)

    def arrive(index):
        pl.when(moves[index][4])(copies[index].wait_recv)

    def leave(index):
        pl.when(moves[index][3])(copies[index].wait_send)

    for index in range(8):
        if index < 6:
            target = moves[index][1]

            @pl.when(jnp.logical_not(moves[index][4]))
            def _(target=target):
                target[...] = jnp.zeros(target.shape, target.dtype)

        else:
            target = rim_in.at[index - 6]

            @pl.when(jnp.logical_not(moves[index][4]))
            def _(target=target):
                target[...] = jnp.zeros(target.shape, target.dtype)

    sums[...] = jnp.zeros_like(sums)
    for row in range(taps):
        time_back[:, row * channels : (row + 1) * channels] = time_ref[
            row * channels : (row + 1) * channels, :
        ]
        time_back[:, (taps + row) * channels : (taps + row + 1) * channels] = time_ref[
            row * channels : (row + 1) * channels, :
        ]
        for col in range(taps):
            index = row * taps + col
            weight = space_ref[index * channels : (index + 1) * channels, :]
            space_fwd[
                row * channels : (row + 1) * channels, col * channels : (col + 1) * channels
            ] = weight
            space_back[:, index * channels : (index + 1) * channels] = weight

    pl.semaphore_wait(barrier, tiles + shards - 2)
    for index in range(4):
        launch(index)
    place = columns(plane, width, channels)

    def window(frame):
        return jnp.concatenate(
            [flat(cells[frame, pl.ds(row, height)]) for row in range(taps)], axis=1
        )

    loads[0].wait()
    arrive(0)
    arrive(1)

    def convolve(frame):
        parts = jnp.dot(window(frame), space_fwd[...], preferred_element_type=jnp.float32)
        value = (
            before(parts[:, :channels], place)
            + parts[:, channels : 2 * channels]
            + after(parts[:, 2 * channels :], place, width)
        )
        pre[frame] = value
        act = value / (1.0 + jnp.exp(-value))
        acts[frame + 2] = act.astype(jnp.bfloat16).reshape(height, width, channels)

    frames(0, count, convolve)
    loads[1].wait()
    loads[2].wait()
    leave(2)
    leave(3)
    launch(4)
    launch(5)
    arrive(2)
    arrive(3)

    def backward(frame):
        joined = jnp.concatenate(
            [flat(cot_f[frame + lag]) for lag in range(taps)]
            + [flat(cot_r[frame + 2 - lag]) for lag in range(taps)],
            axis=1,
        )
        grad_act = across(joined, time_back[...])
        value = pre[frame]
        gate = 1.0 / (1.0 + jnp.exp(-value))
        grad = grad_act * gate * (1.0 + value * (1.0 - gate))
        grad = grad.astype(jnp.bfloat16).astype(jnp.float32)
        shifted = spread(grad, place, width)
        wide[frame, pl.ds(1, height)] = shifted.reshape(height, width, taps * channels)
        rounded = grad.astype(jnp.bfloat16)
        rim_out[0, frame] = rounded[:width]
        rim_out[1, frame] = rounded[plane - width :]
        lags = contract(flat(acts[frame + 2]), joined)
        for lag in range(taps):
            row = (taps * taps + lag) * channels
            sums[row : row + channels, :] += (
                lags[:, lag * channels : (lag + 1) * channels]
                + lags[:, (taps + lag) * channels : (taps + lag + 1) * channels]
            )
        part = contract(window(frame), shifted)
        for row in range(taps):
            for col in range(taps):
                start = (row * taps + col) * channels
                sums[start : start + channels, :] += part[
                    row * channels : (row + 1) * channels, col * channels : (col + 1) * channels
                ]

    frames(0, count, backward)
    launch(6)
    launch(7)

    half = sums.shape[0] // tiles
    chunk = half // shards

    def settle(phase, ref):
        pltpu.make_async_copy(ref, ref, send_sem.at[phase]).wait()
        pltpu.make_async_copy(ref, ref, recv_sem.at[phase]).wait()

    def rows_to(step):
        return lax.rem(tile + step, tiles) * half

    pair_out[...] = sums[...].astype(PAIR_WIRE)
    each(
        tiles,
        lambda step: remote(
            pair_out.at[at(rows_to(step), half)], pair_in.at[step - 1], 8, tile_peer(step)
        ).start(),
    )

    def outputs(frame):
        base = flat(cells[frame, pl.ds(1, height)]).astype(jnp.float32)
        causal = jnp.concatenate([flat(acts[frame + 2 - lag]) for lag in range(taps)], axis=1)
        anticausal = jnp.concatenate([flat(acts[frame + 2 + lag]) for lag in range(taps)], axis=1)
        for joined, ref in ((causal, out_f), (anticausal, out_r)):
            value = base + jnp.dot(joined, time_ref[...], preferred_element_type=jnp.float32)
            ref[frame] = value.astype(jnp.bfloat16).reshape(height, width, channels)

    def input_grads(frame):
        joined = jnp.concatenate(
            [flat(wide[frame, pl.ds(2 - row, height)]) for row in range(taps)], axis=1
        )
        value = flat(cot_f[frame]).astype(jnp.float32) + flat(cot_r[frame + 2]).astype(jnp.float32)
        value = value + across(joined, space_back[...])
        grad_in[frame] = value.astype(jnp.bfloat16).reshape(height, width, channels)

    stores = [
        pltpu.make_async_copy(src, dst, store_sem.at[index])
        for index, (src, dst) in enumerate(
            (
                (out_f, out_f_ref),
                (out_r, out_r_ref),
                (grad_in, grad_in_ref),
                (grad_s, grad_s_ref),
                (grad_t, grad_t_ref),
            )
        )
    ]
    settle(8, pair_in)
    own_half = sums[at(tile * half, half), :]
    for index in range(tiles - 1):
        own_half = own_half + pair_in[index].astype(jnp.float32)
    mid[...] = own_half
    mid_out[...] = own_half.astype(PART_WIRE)
    each(
        shards,
        lambda step: remote(
            mid_out.at[at(lax.rem(shard + step, shards) * chunk, chunk)],
            shard_in.at[step - 1],
            9,
            shard_peer(step),
        ).start(),
    )
    arrive(4)
    arrive(5)
    frames(0, count, outputs)
    stores[0].start()
    stores[1].start()
    settle(9, shard_in)
    part = lax.fori_loop(
        0,
        shards - 1,
        lambda index, value: value + shard_in[index].astype(jnp.float32),
        mid[at(shard * chunk, chunk), :],
    )
    own = at(tile * half + shard * chunk, chunk)
    total[own, :] = (part * scale).astype(SUM_WIRE)
    each(
        shards,
        lambda step: remote(total.at[own], total.at[own], 10, shard_peer(step)).start(),
    )
    arrive(6)
    arrive(7)
    edge = columns(count * width, width, channels)
    for side, row in ((0, 0), (1, height + 1)):
        rim = spread(flat(rim_in[side]).astype(jnp.float32), edge, width)
        wide[:, row] = rim.reshape(count, width, taps * channels)
    frames(0, count, input_grads)
    stores[2].start()
    settle(10, total.at[pl.ds(0, (shards - 1) * chunk)])
    mine = at(tile * half, half)
    each(
        tiles,
        lambda step: remote(total.at[mine], total.at[mine], 11, tile_peer(step)).start(),
    )
    for index in (0, 1, 4, 5, 6, 7):
        leave(index)
    settle(11, total.at[pl.ds(0, (tiles - 1) * half)])
    split = taps * taps * channels
    grad_s[...] = total[:split, :].astype(jnp.float32)
    stores[3].start()
    grad_t[...] = total[split : split + taps * channels, :].astype(jnp.float32)
    stores[4].start()
    for store in stores:
        store.wait()


def deliver_kernel(*refs):
    count = (len(refs) - 2) // 3
    sources, targets, held = refs[:count], refs[count : 2 * count], refs[2 * count : 3 * count]
    load_sem, store_sem = refs[3 * count :]
    loads, stores = [], []
    for index in range(count):
        loads.append(pltpu.make_async_copy(sources[index], held[index], load_sem.at[index]))
        stores.append(pltpu.make_async_copy(held[index], targets[index], store_sem.at[index]))
    for load in loads:
        load.start()
    for load, store in zip(loads, stores):
        load.wait()
        store.start()
    for store in stores:
        store.wait()


def deliver(*values):
    hbm = pl.BlockSpec(memory_space=pl.ANY)
    count = len(values)
    return pl.pallas_call(
        deliver_kernel,
        out_shape=tuple(jax.ShapeDtypeStruct(value.shape, value.dtype) for value in values),
        in_specs=[hbm] * count,
        out_specs=(hbm,) * count,
        scratch_shapes=[pltpu.VMEM(value.shape, value.dtype) for value in values]
        + [pltpu.SemaphoreType.DMA((count,)), pltpu.SemaphoreType.DMA((count,))],
    )(*values)


def body(latent, cot_forward, cot_reverse, spatial_weight, temporal_weight):
    tiles, shards = lax.axis_size("tile"), lax.axis_size("tm")
    count, height, width, channels = latent.shape
    positions = count * height * width * shards * tiles
    scale = 1.0 / math.sqrt(positions)
    rows = 12 * channels
    unit = 16 * tiles * shards
    padded = -(-rows // unit) * unit
    half = padded // tiles
    chunk = half // shards
    kind = jnp.bfloat16
    vmem = pl.BlockSpec(memory_space=pltpu.VMEM)
    hbm = pl.BlockSpec(memory_space=pl.ANY)
    results = pl.pallas_call(
        functools.partial(kernel, tiles, shards, scale),
        out_shape=(
            jax.ShapeDtypeStruct(latent.shape, kind),
            jax.ShapeDtypeStruct(latent.shape, kind),
            jax.ShapeDtypeStruct(latent.shape, kind),
            jax.ShapeDtypeStruct((9 * channels, channels), jnp.float32),
            jax.ShapeDtypeStruct((3 * channels, channels), jnp.float32),
        ),
        in_specs=[hbm, hbm, hbm, vmem, vmem],
        out_specs=(hbm, hbm, hbm, hbm, hbm),
        scratch_shapes=[
            pltpu.VMEM((count, height + 2, width, channels), kind),
            pltpu.VMEM((count + 2, height, width, channels), kind),
            pltpu.VMEM((count + 2, height, width, channels), kind),
            pltpu.VMEM((count + 4, height, width, channels), kind),
            pltpu.VMEM((count, height * width, channels), jnp.float32),
            pltpu.VMEM((count, height + 2, width, 3 * channels), kind),
            pltpu.VMEM((2, count, width, channels), kind),
            pltpu.VMEM((2, count, width, channels), kind),
            pltpu.VMEM((3 * channels, 3 * channels), kind),
            pltpu.VMEM((channels, 9 * channels), kind),
            pltpu.VMEM((channels, 6 * channels), kind),
            pltpu.VMEM((padded, channels), jnp.float32),
            pltpu.VMEM((padded, channels), PAIR_WIRE),
            pltpu.VMEM((tiles - 1, half, channels), PAIR_WIRE),
            pltpu.VMEM((half, channels), jnp.float32),
            pltpu.VMEM((half, channels), PART_WIRE),
            pltpu.VMEM((shards - 1, chunk, channels), PART_WIRE),
            pltpu.VMEM((padded, channels), SUM_WIRE),
            pltpu.VMEM(latent.shape, kind),
            pltpu.VMEM(latent.shape, kind),
            pltpu.VMEM(latent.shape, kind),
            pltpu.VMEM((9 * channels, channels), jnp.float32),
            pltpu.VMEM((3 * channels, channels), jnp.float32),
            pltpu.SemaphoreType.DMA((3,)),
            pltpu.SemaphoreType.DMA((5,)),
            pltpu.SemaphoreType.DMA((12,)),
            pltpu.SemaphoreType.DMA((12,)),
        ],
        compiler_params=pltpu.CompilerParams(collective_id=0, has_side_effects=True),
    )(
        latent,
        cot_forward,
        cot_reverse,
        spatial_weight.reshape(9 * channels, channels),
        temporal_weight.reshape(3 * channels, channels),
    )
    out_f, out_r, grad_in, grad_s, grad_t = deliver(*results)
    return (
        out_f,
        out_r,
        grad_in,
        grad_s.reshape(spatial_weight.shape),
        grad_t.reshape(temporal_weight.shape),
    )


def solution(mesh):
    placed = (
        P("tm", "tile", None, None),
        P("tm", "tile", None, None),
        P("tm", "tile", None, None),
        P(),
        P(),
    )
    return jax.shard_map(
        body,
        mesh=mesh,
        in_specs=placed,
        out_specs=(
            P("tm", "tile", None, None),
            P("tm", "tile", None, None),
            P("tm", "tile", None, None),
            P(),
            P(),
        ),
        check_vma=False,
    )
```

```python
import functools
import math

import jax
import jax.numpy as jnp
from jax import lax
from jax.experimental import pallas as pl
from jax.experimental.pallas import tpu as pltpu
from jax.sharding import PartitionSpec as P

MESH = pl.DeviceIdType.MESH
PAIR_WIRE = jnp.float32
PART_WIRE = jnp.float32
SUM_WIRE = jnp.bfloat16
FIRST = 0
MOMENT = 2
LATE_OUT = False


def at(start, size):
    return pl.ds(pl.multiple_of(start, 16), size)


def each(count, act):
    def step(index, carry):
        act(index)
        return carry

    lax.fori_loop(1, count, step, 0)


def frames(first, last, act):
    def step(index, carry):
        act(index)
        return carry

    lax.fori_loop(first, last, step, 0)


def columns(rows, width, channels):
    place = lax.broadcasted_iota(jnp.int32, (rows // width, width, channels), 1)
    return place.reshape(rows, channels)


def before(value, place):
    return jnp.where(place == 0, 0.0, pltpu.roll(value, 1, 0))


def after(value, place, width):
    return jnp.where(place == width - 1, 0.0, pltpu.roll(value, value.shape[0] - 1, 0))


def spread(value, place, width):
    kind = jnp.bfloat16
    return jnp.concatenate(
        [after(value, place, width).astype(kind), value.astype(kind), before(value, place).astype(kind)],
        axis=1,
    )


def flat(value):
    return value.reshape(-1, value.shape[-1])


def across(left, right):
    return lax.dot_general(
        left, right, (((1,), (1,)), ((), ())), preferred_element_type=jnp.float32
    )


def contract(left, right):
    return lax.dot_general(
        left, right, (((0,), (0,)), ((), ())), preferred_element_type=jnp.float32
    )


def kernel(
    tiles,
    shards,
    scale,
    latent_ref,
    fwd_ref,
    rev_ref,
    space_ref,
    time_ref,
    out_f_ref,
    out_r_ref,
    grad_in_ref,
    grad_s_ref,
    grad_t_ref,
    cells,
    cot_f,
    cot_r,
    acts,
    pre,
    wide,
    rim_out,
    rim_in,
    space_fwd,
    space_back,
    time_back,
    sums,
    pair_out,
    pair_in,
    mid,
    mid_out,
    shard_in,
    total,
    out_f,
    out_r,
    grad_in,
    grad_s,
    grad_t,
    load_sem,
    store_sem,
    send_sem,
    recv_sem,
):
    tile, shard = lax.axis_index("tile"), lax.axis_index("tm")
    count, height, width, channels = latent_ref.shape
    plane = height * width
    taps = 3

    def tile_peer(step):
        return {"tile": lax.rem(tile + step, tiles)}

    def shard_peer(step):
        return {"tm": lax.rem(shard + step, shards)}

    barrier = pltpu.get_barrier_semaphore()

    def greet(peer):
        pl.semaphore_signal(barrier, inc=1, device_id=peer, device_id_type=MESH)

    each(tiles, lambda step: greet(tile_peer(step)))
    each(shards, lambda step: greet(shard_peer(step)))

    loads = [
        pltpu.make_async_copy(latent_ref, cells.at[:, pl.ds(1, height)], load_sem.at[0]),
        pltpu.make_async_copy(fwd_ref, cot_f.at[pl.ds(0, count)], load_sem.at[1]),
        pltpu.make_async_copy(rev_ref, cot_r.at[pl.ds(2, count)], load_sem.at[2]),
    ]
    for load in loads:
        load.start()

    has_next_tile, has_last_tile = tile < tiles - 1, tile > 0
    has_next_shard, has_last_shard = shard < shards - 1, shard > 0

    def remote(src, dst, index, peer):
        return pltpu.make_async_remote_copy(
            src_ref=src,
            dst_ref=dst,
            send_sem=send_sem.at[index],
            recv_sem=recv_sem.at[index],
            device_id=peer,
            device_id_type=MESH,
        )

    next_tile, last_tile = tile_peer(1), tile_peer(tiles - 1)
    next_shard, last_shard = shard_peer(1), shard_peer(shards - 1)
    up = (next_tile, has_next_tile, has_last_tile)
    down = (last_tile, has_last_tile, has_next_tile)
    later = (next_shard, has_next_shard, has_last_shard)
    earlier = (last_shard, has_last_shard, has_next_shard)
    moves = [
        (latent_ref.at[:, height - 1], cells.at[:, 0], *up),
        (latent_ref.at[:, 0], cells.at[:, height + 1], *down),
        (fwd_ref.at[0], cot_f.at[count], *earlier),
        (rev_ref.at[count - 1], cot_r.at[1], *later),
        (fwd_ref.at[1], cot_f.at[count + 1], *earlier),
        (rev_ref.at[count - 2], cot_r.at[0], *later),
        (acts.at[count + 1], acts.at[1], *later),
        (acts.at[2], acts.at[count + 2], *earlier),
        (acts.at[count], acts.at[0], *later),
        (acts.at[3], acts.at[count + 3], *earlier),
        (rim_out.at[1], rim_in.at[0], *up),
        (rim_out.at[0], rim_in.at[1], *down),
    ]
    copies = [remote(src, dst, index, peer) for index, (src, dst, peer, _, _) in enumerate(moves)]

    def launch(index):
        pl.when(moves[index][3])(copies[index].start)

    def arrive(index):
        pl.when(moves[index][4])(copies[index].wait_recv)

    def leave(index):
        pl.when(moves[index][3])(copies[index].wait_send)

    for index in range(len(moves)):
        target = moves[index][1]

        @pl.when(jnp.logical_not(moves[index][4]))
        def _(target=target):
            target[...] = jnp.zeros(target.shape, target.dtype)

    sums[...] = jnp.zeros_like(sums)
    for row in range(taps):
        time_back[:, row * channels : (row + 1) * channels] = time_ref[
            row * channels : (row + 1) * channels, :
        ]
        time_back[:, (taps + row) * channels : (taps + row + 1) * channels] = time_ref[
            row * channels : (row + 1) * channels, :
        ]
        for col in range(taps):
            index = row * taps + col
            weight = space_ref[index * channels : (index + 1) * channels, :]
            space_fwd[
                row * channels : (row + 1) * channels, col * channels : (col + 1) * channels
            ] = weight
            space_back[:, index * channels : (index + 1) * channels] = weight

    pl.semaphore_wait(barrier, tiles + shards - 2)
    for index in range(6):
        launch(index)
    place = columns(plane, width, channels)

    def window(frame):
        return jnp.concatenate(
            [flat(cells[frame, pl.ds(row, height)]) for row in range(taps)], axis=1
        )

    loads[0].wait()
    arrive(0)
    arrive(1)

    def convolve(frame):
        parts = jnp.dot(window(frame), space_fwd[...], preferred_element_type=jnp.float32)
        value = (
            before(parts[:, :channels], place)
            + parts[:, channels : 2 * channels]
            + after(parts[:, 2 * channels :], place, width)
        )
        pre[frame] = value
        act = value / (1.0 + jnp.exp(-value))
        acts[frame + 2] = act.astype(jnp.bfloat16).reshape(height, width, channels)

    frames(0, count, convolve)

    def second_acts(moment):
        if moment == FIRST:
            launch(6)
            launch(7)
        if moment == MOMENT:
            launch(8)
            launch(9)

    def backward(frame):
        joined = jnp.concatenate(
            [flat(cot_f[frame + lag]) for lag in range(taps)]
            + [flat(cot_r[frame + 2 - lag]) for lag in range(taps)],
            axis=1,
        )
        grad_act = across(joined, time_back[...])
        value = pre[frame]
        gate = 1.0 / (1.0 + jnp.exp(-value))
        grad = grad_act * gate * (1.0 + value * (1.0 - gate))
        grad = grad.astype(jnp.bfloat16).astype(jnp.float32)
        shifted = spread(grad, place, width)
        wide[frame, pl.ds(1, height)] = shifted.reshape(height, width, taps * channels)
        rounded = grad.astype(jnp.bfloat16)
        rim_out[0, frame] = rounded[:width]
        rim_out[1, frame] = rounded[plane - width :]
        lags = contract(flat(acts[frame + 2]), joined)
        for lag in range(taps):
            row = (taps * taps + lag) * channels
            sums[row : row + channels, :] += (
                lags[:, lag * channels : (lag + 1) * channels]
                + lags[:, (taps + lag) * channels : (taps + lag + 1) * channels]
            )
        part = contract(window(frame), shifted)
        for row in range(taps):
            for col in range(taps):
                start = (row * taps + col) * channels
                sums[start : start + channels, :] += part[
                    row * channels : (row + 1) * channels, col * channels : (col + 1) * channels
                ]

    loads[1].wait()
    loads[2].wait()
    arrive(2)
    arrive(3)
    frames(1, count - 1, backward)
    for index in (2, 3, 4, 5):
        leave(index)
    second_acts(0)
    arrive(4)
    arrive(5)
    backward(0)
    backward(count - 1)
    launch(10)
    launch(11)

    half = sums.shape[0] // tiles
    chunk = half // shards

    def settle(phase, ref):
        pltpu.make_async_copy(ref, ref, send_sem.at[phase]).wait()
        pltpu.make_async_copy(ref, ref, recv_sem.at[phase]).wait()

    def rows_to(step):
        return lax.rem(tile + step, tiles) * half

    pair_out[...] = sums[...].astype(PAIR_WIRE)
    each(
        tiles,
        lambda step: remote(
            pair_out.at[at(rows_to(step), half)], pair_in.at[step - 1], 12, tile_peer(step)
        ).start(),
    )

    second_acts(1)

    def outputs(frame):
        base = flat(cells[frame, pl.ds(1, height)]).astype(jnp.float32)
        causal = jnp.concatenate([flat(acts[frame + 2 - lag]) for lag in range(taps)], axis=1)
        anticausal = jnp.concatenate([flat(acts[frame + 2 + lag]) for lag in range(taps)], axis=1)
        for joined, ref in ((causal, out_f), (anticausal, out_r)):
            value = base + jnp.dot(joined, time_ref[...], preferred_element_type=jnp.float32)
            ref[frame] = value.astype(jnp.bfloat16).reshape(height, width, channels)

    def all_outputs():
        for index in range(6, 10):
            arrive(index)
        frames(0, count, outputs)
        stores[0].start()
        stores[1].start()

    def input_grads(frame):
        joined = jnp.concatenate(
            [flat(wide[frame, pl.ds(2 - row, height)]) for row in range(taps)], axis=1
        )
        value = flat(cot_f[frame]).astype(jnp.float32) + flat(cot_r[frame + 2]).astype(jnp.float32)
        value = value + across(joined, space_back[...])
        grad_in[frame] = value.astype(jnp.bfloat16).reshape(height, width, channels)

    stores = [
        pltpu.make_async_copy(src, dst, store_sem.at[index])
        for index, (src, dst) in enumerate(
            (
                (out_f, out_f_ref),
                (out_r, out_r_ref),
                (grad_in, grad_in_ref),
                (grad_s, grad_s_ref),
                (grad_t, grad_t_ref),
            )
        )
    ]
    settle(12, pair_in)
    own_half = sums[at(tile * half, half), :]
    for index in range(tiles - 1):
        own_half = own_half + pair_in[index].astype(jnp.float32)
    mid[...] = own_half
    mid_out[...] = own_half.astype(PART_WIRE)
    each(
        shards,
        lambda step: remote(
            mid_out.at[at(lax.rem(shard + step, shards) * chunk, chunk)],
            shard_in.at[step - 1],
            13,
            shard_peer(step),
        ).start(),
    )
    second_acts(2)
    settle(13, shard_in)
    part = lax.fori_loop(
        0,
        shards - 1,
        lambda index, value: value + shard_in[index].astype(jnp.float32),
        mid[at(shard * chunk, chunk), :],
    )
    own = at(tile * half + shard * chunk, chunk)
    total[own, :] = (part * scale).astype(SUM_WIRE)
    each(
        shards,
        lambda step: remote(total.at[own], total.at[own], 14, shard_peer(step)).start(),
    )
    second_acts(3)
    arrive(10)
    arrive(11)
    edge = columns(count * width, width, channels)
    for side, row in ((0, 0), (1, height + 1)):
        rim = spread(flat(rim_in[side]).astype(jnp.float32), edge, width)
        wide[:, row] = rim.reshape(count, width, taps * channels)
    frames(0, count, input_grads)
    stores[2].start()
    if not LATE_OUT:
        all_outputs()
    settle(14, total.at[pl.ds(0, (shards - 1) * chunk)])
    mine = at(tile * half, half)
    each(
        tiles,
        lambda step: remote(total.at[mine], total.at[mine], 15, tile_peer(step)).start(),
    )
    if LATE_OUT:
        all_outputs()
    for index in (0, 1, 6, 7, 8, 9, 10, 11):
        leave(index)
    settle(15, total.at[pl.ds(0, (tiles - 1) * half)])
    split = taps * taps * channels
    grad_s[...] = total[:split, :].astype(jnp.float32)
    stores[3].start()
    grad_t[...] = total[split : split + taps * channels, :].astype(jnp.float32)
    stores[4].start()
    for store in stores:
        store.wait()


def deliver_kernel(*refs):
    count = (len(refs) - 2) // 3
    sources, targets, held = refs[:count], refs[count : 2 * count], refs[2 * count : 3 * count]
    load_sem, store_sem = refs[3 * count :]
    loads, stores = [], []
    for index in range(count):
        loads.append(pltpu.make_async_copy(sources[index], held[index], load_sem.at[index]))
        stores.append(pltpu.make_async_copy(held[index], targets[index], store_sem.at[index]))
    for load in loads:
        load.start()
    for load, store in zip(loads, stores):
        load.wait()
        store.start()
    for store in stores:
        store.wait()


def deliver(*values):
    hbm = pl.BlockSpec(memory_space=pl.ANY)
    count = len(values)
    return pl.pallas_call(
        deliver_kernel,
        out_shape=tuple(jax.ShapeDtypeStruct(value.shape, value.dtype) for value in values),
        in_specs=[hbm] * count,
        out_specs=(hbm,) * count,
        scratch_shapes=[pltpu.VMEM(value.shape, value.dtype) for value in values]
        + [pltpu.SemaphoreType.DMA((count,)), pltpu.SemaphoreType.DMA((count,))],
    )(*values)


def body(latent, cot_forward, cot_reverse, spatial_weight, temporal_weight):
    tiles, shards = lax.axis_size("tile"), lax.axis_size("tm")
    count, height, width, channels = latent.shape
    positions = count * height * width * shards * tiles
    scale = 1.0 / math.sqrt(positions)
    rows = 12 * channels
    unit = 16 * tiles * shards
    padded = -(-rows // unit) * unit
    half = padded // tiles
    chunk = half // shards
    kind = jnp.bfloat16
    vmem = pl.BlockSpec(memory_space=pltpu.VMEM)
    hbm = pl.BlockSpec(memory_space=pl.ANY)
    results = pl.pallas_call(
        functools.partial(kernel, tiles, shards, scale),
        out_shape=(
            jax.ShapeDtypeStruct(latent.shape, kind),
            jax.ShapeDtypeStruct(latent.shape, kind),
            jax.ShapeDtypeStruct(latent.shape, kind),
            jax.ShapeDtypeStruct((9 * channels, channels), jnp.float32),
            jax.ShapeDtypeStruct((3 * channels, channels), jnp.float32),
        ),
        in_specs=[hbm, hbm, hbm, vmem, vmem],
        out_specs=(hbm, hbm, hbm, hbm, hbm),
        scratch_shapes=[
            pltpu.VMEM((count, height + 2, width, channels), kind),
            pltpu.VMEM((count + 2, height, width, channels), kind),
            pltpu.VMEM((count + 2, height, width, channels), kind),
            pltpu.VMEM((count + 4, height, width, channels), kind),
            pltpu.VMEM((count, height * width, channels), jnp.float32),
            pltpu.VMEM((count, height + 2, width, 3 * channels), kind),
            pltpu.VMEM((2, count, width, channels), kind),
            pltpu.VMEM((2, count, width, channels), kind),
            pltpu.VMEM((3 * channels, 3 * channels), kind),
            pltpu.VMEM((channels, 9 * channels), kind),
            pltpu.VMEM((channels, 6 * channels), kind),
            pltpu.VMEM((padded, channels), jnp.float32),
            pltpu.VMEM((padded, channels), PAIR_WIRE),
            pltpu.VMEM((tiles - 1, half, channels), PAIR_WIRE),
            pltpu.VMEM((half, channels), jnp.float32),
            pltpu.VMEM((half, channels), PART_WIRE),
            pltpu.VMEM((shards - 1, chunk, channels), PART_WIRE),
            pltpu.VMEM((padded, channels), SUM_WIRE),
            pltpu.VMEM(latent.shape, kind),
            pltpu.VMEM(latent.shape, kind),
            pltpu.VMEM(latent.shape, kind),
            pltpu.VMEM((9 * channels, channels), jnp.float32),
            pltpu.VMEM((3 * channels, channels), jnp.float32),
            pltpu.SemaphoreType.DMA((3,)),
            pltpu.SemaphoreType.DMA((5,)),
            pltpu.SemaphoreType.DMA((16,)),
            pltpu.SemaphoreType.DMA((16,)),
        ],
        compiler_params=pltpu.CompilerParams(collective_id=0, has_side_effects=True),
    )(
        latent,
        cot_forward,
        cot_reverse,
        spatial_weight.reshape(9 * channels, channels),
        temporal_weight.reshape(3 * channels, channels),
    )
    out_f, out_r, grad_in, grad_s, grad_t = deliver(*results)
    return (
        out_f,
        out_r,
        grad_in,
        grad_s.reshape(spatial_weight.shape),
        grad_t.reshape(temporal_weight.shape),
    )


def solution(mesh):
    placed = (
        P("tm", "tile", None, None),
        P("tm", "tile", None, None),
        P("tm", "tile", None, None),
        P(),
        P(),
    )
    return jax.shard_map(
        body,
        mesh=mesh,
        in_specs=placed,
        out_specs=(
            P("tm", "tile", None, None),
            P("tm", "tile", None, None),
            P("tm", "tile", None, None),
            P(),
            P(),
        ),
        check_vma=False,
    )
```

```python
import functools
import math

import jax
import jax.numpy as jnp
from jax import lax
from jax.experimental import pallas as pl
from jax.experimental.pallas import tpu as pltpu
from jax.sharding import PartitionSpec as P

MESH = pl.DeviceIdType.MESH
PAIR_WIRE = jnp.float32
PART_WIRE = jnp.bfloat16
SUM_WIRE = jnp.bfloat16
FIRST = 0
MOMENT = 2
LATE_OUT = False


def at(start, size):
    return pl.ds(pl.multiple_of(start, 16), size)


def each(count, act):
    def step(index, carry):
        act(index)
        return carry

    lax.fori_loop(1, count, step, 0)


def frames(first, last, act):
    def step(index, carry):
        act(index)
        return carry

    lax.fori_loop(first, last, step, 0)


def columns(rows, width, channels):
    place = lax.broadcasted_iota(jnp.int32, (rows // width, width, channels), 1)
    return place.reshape(rows, channels)


def before(value, place):
    return jnp.where(place == 0, 0.0, pltpu.roll(value, 1, 0))


def after(value, place, width):
    return jnp.where(place == width - 1, 0.0, pltpu.roll(value, value.shape[0] - 1, 0))


def spread(value, place, width):
    kind = jnp.bfloat16
    return jnp.concatenate(
        [after(value, place, width).astype(kind), value.astype(kind), before(value, place).astype(kind)],
        axis=1,
    )


def flat(value):
    return value.reshape(-1, value.shape[-1])


def across(left, right):
    return lax.dot_general(
        left, right, (((1,), (1,)), ((), ())), preferred_element_type=jnp.float32
    )


def contract(left, right):
    return lax.dot_general(
        left, right, (((0,), (0,)), ((), ())), preferred_element_type=jnp.float32
    )


def kernel(
    tiles,
    shards,
    scale,
    latent_ref,
    fwd_ref,
    rev_ref,
    space_ref,
    time_ref,
    out_f_ref,
    out_r_ref,
    grad_in_ref,
    grad_s_ref,
    grad_t_ref,
    cells,
    cot_f,
    cot_r,
    acts,
    pre,
    wide,
    rim_out,
    rim_in,
    space_fwd,
    space_back,
    time_back,
    sums,
    pair_out,
    pair_in,
    mid,
    mid_out,
    shard_in,
    total,
    out_f,
    out_r,
    grad_in,
    grad_s,
    grad_t,
    load_sem,
    store_sem,
    send_sem,
    recv_sem,
):
    tile, shard = lax.axis_index("tile"), lax.axis_index("tm")
    count, height, width, channels = latent_ref.shape
    plane = height * width
    taps = 3

    def tile_peer(step):
        return {"tile": lax.rem(tile + step, tiles)}

    def shard_peer(step):
        return {"tm": lax.rem(shard + step, shards)}

    barrier = pltpu.get_barrier_semaphore()

    def greet(peer):
        pl.semaphore_signal(barrier, inc=1, device_id=peer, device_id_type=MESH)

    each(tiles, lambda step: greet(tile_peer(step)))
    each(shards, lambda step: greet(shard_peer(step)))

    loads = [
        pltpu.make_async_copy(latent_ref, cells.at[:, pl.ds(1, height)], load_sem.at[0]),
        pltpu.make_async_copy(fwd_ref, cot_f.at[pl.ds(0, count)], load_sem.at[1]),
        pltpu.make_async_copy(rev_ref, cot_r.at[pl.ds(2, count)], load_sem.at[2]),
    ]
    for load in loads:
        load.start()

    has_next_tile, has_last_tile = tile < tiles - 1, tile > 0
    has_next_shard, has_last_shard = shard < shards - 1, shard > 0

    def remote(src, dst, index, peer):
        return pltpu.make_async_remote_copy(
            src_ref=src,
            dst_ref=dst,
            send_sem=send_sem.at[index],
            recv_sem=recv_sem.at[index],
            device_id=peer,
            device_id_type=MESH,
        )

    next_tile, last_tile = tile_peer(1), tile_peer(tiles - 1)
    next_shard, last_shard = shard_peer(1), shard_peer(shards - 1)
    up = (next_tile, has_next_tile, has_last_tile)
    down = (last_tile, has_last_tile, has_next_tile)
    later = (next_shard, has_next_shard, has_last_shard)
    earlier = (last_shard, has_last_shard, has_next_shard)
    moves = [
        (latent_ref.at[:, height - 1], cells.at[:, 0], *up),
        (latent_ref.at[:, 0], cells.at[:, height + 1], *down),
        (fwd_ref.at[0], cot_f.at[count], *earlier),
        (rev_ref.at[count - 1], cot_r.at[1], *later),
        (fwd_ref.at[1], cot_f.at[count + 1], *earlier),
        (rev_ref.at[count - 2], cot_r.at[0], *later),
        (acts.at[count + 1], acts.at[1], *later),
        (acts.at[2], acts.at[count + 2], *earlier),
        (acts.at[count], acts.at[0], *later),
        (acts.at[3], acts.at[count + 3], *earlier),
        (rim_out.at[1], rim_in.at[0], *up),
        (rim_out.at[0], rim_in.at[1], *down),
    ]
    copies = [remote(src, dst, index, peer) for index, (src, dst, peer, _, _) in enumerate(moves)]

    def launch(index):
        pl.when(moves[index][3])(copies[index].start)

    def arrive(index):
        pl.when(moves[index][4])(copies[index].wait_recv)

    def leave(index):
        pl.when(moves[index][3])(copies[index].wait_send)

    for index in range(len(moves)):
        target = moves[index][1]

        @pl.when(jnp.logical_not(moves[index][4]))
        def _(target=target):
            target[...] = jnp.zeros(target.shape, target.dtype)

    sums[...] = jnp.zeros_like(sums)
    for row in range(taps):
        time_back[:, row * channels : (row + 1) * channels] = time_ref[
            row * channels : (row + 1) * channels, :
        ]
        time_back[:, (taps + row) * channels : (taps + row + 1) * channels] = time_ref[
            row * channels : (row + 1) * channels, :
        ]
        for col in range(taps):
            index = row * taps + col
            weight = space_ref[index * channels : (index + 1) * channels, :]
            space_fwd[
                row * channels : (row + 1) * channels, col * channels : (col + 1) * channels
            ] = weight
            space_back[:, index * channels : (index + 1) * channels] = weight

    pl.semaphore_wait(barrier, tiles + shards - 2)
    for index in range(6):
        launch(index)
    place = columns(plane, width, channels)

    def window(frame):
        return jnp.concatenate(
            [flat(cells[frame, pl.ds(row, height)]) for row in range(taps)], axis=1
        )

    loads[0].wait()
    arrive(0)
    arrive(1)

    def convolve(frame):
        parts = jnp.dot(window(frame), space_fwd[...], preferred_element_type=jnp.float32)
        value = (
            before(parts[:, :channels], place)
            + parts[:, channels : 2 * channels]
            + after(parts[:, 2 * channels :], place, width)
        )
        pre[frame] = value
        act = value / (1.0 + jnp.exp(-value))
        acts[frame + 2] = act.astype(jnp.bfloat16).reshape(height, width, channels)

    frames(0, count, convolve)

    def second_acts(moment):
        if moment == FIRST:
            launch(6)
            launch(7)
        if moment == MOMENT:
            launch(8)
            launch(9)

    def backward(frame):
        joined = jnp.concatenate(
            [flat(cot_f[frame + lag]) for lag in range(taps)]
            + [flat(cot_r[frame + 2 - lag]) for lag in range(taps)],
            axis=1,
        )
        grad_act = across(joined, time_back[...])
        value = pre[frame]
        gate = 1.0 / (1.0 + jnp.exp(-value))
        grad = grad_act * gate * (1.0 + value * (1.0 - gate))
        grad = grad.astype(jnp.bfloat16).astype(jnp.float32)
        shifted = spread(grad, place, width)
        wide[frame, pl.ds(1, height)] = shifted.reshape(height, width, taps * channels)
        rounded = grad.astype(jnp.bfloat16)
        rim_out[0, frame] = rounded[:width]
        rim_out[1, frame] = rounded[plane - width :]
        lags = contract(flat(acts[frame + 2]), joined)
        for lag in range(taps):
            row = (taps * taps + lag) * channels
            sums[row : row + channels, :] += (
                lags[:, lag * channels : (lag + 1) * channels]
                + lags[:, (taps + lag) * channels : (taps + lag + 1) * channels]
            )
        part = contract(window(frame), shifted)
        for row in range(taps):
            for col in range(taps):
                start = (row * taps + col) * channels
                sums[start : start + channels, :] += part[
                    row * channels : (row + 1) * channels, col * channels : (col + 1) * channels
                ]

    loads[1].wait()
    loads[2].wait()
    arrive(2)
    arrive(3)
    frames(1, count - 1, backward)
    for index in (2, 3, 4, 5):
        leave(index)
    second_acts(0)
    arrive(4)
    arrive(5)
    backward(0)
    backward(count - 1)
    launch(10)
    launch(11)

    half = sums.shape[0] // tiles
    chunk = half // shards

    def settle(phase, ref):
        pltpu.make_async_copy(ref, ref, send_sem.at[phase]).wait()
        pltpu.make_async_copy(ref, ref, recv_sem.at[phase]).wait()

    def rows_to(step):
        return lax.rem(tile + step, tiles) * half

    pair_out[...] = sums[...].astype(PAIR_WIRE)
    each(
        tiles,
        lambda step: remote(
            pair_out.at[at(rows_to(step), half)], pair_in.at[step - 1], 12, tile_peer(step)
        ).start(),
    )

    second_acts(1)

    def outputs(frame):
        base = flat(cells[frame, pl.ds(1, height)]).astype(jnp.float32)
        causal = jnp.concatenate([flat(acts[frame + 2 - lag]) for lag in range(taps)], axis=1)
        anticausal = jnp.concatenate([flat(acts[frame + 2 + lag]) for lag in range(taps)], axis=1)
        for joined, ref in ((causal, out_f), (anticausal, out_r)):
            value = base + jnp.dot(joined, time_ref[...], preferred_element_type=jnp.float32)
            ref[frame] = value.astype(jnp.bfloat16).reshape(height, width, channels)

    def all_outputs():
        for index in range(6, 10):
            arrive(index)
        frames(0, count, outputs)
        stores[0].start()
        stores[1].start()

    def input_grads(frame):
        joined = jnp.concatenate(
            [flat(wide[frame, pl.ds(2 - row, height)]) for row in range(taps)], axis=1
        )
        value = flat(cot_f[frame]).astype(jnp.float32) + flat(cot_r[frame + 2]).astype(jnp.float32)
        value = value + across(joined, space_back[...])
        grad_in[frame] = value.astype(jnp.bfloat16).reshape(height, width, channels)

    stores = [
        pltpu.make_async_copy(src, dst, store_sem.at[index])
        for index, (src, dst) in enumerate(
            (
                (out_f, out_f_ref),
                (out_r, out_r_ref),
                (grad_in, grad_in_ref),
                (grad_s, grad_s_ref),
                (grad_t, grad_t_ref),
            )
        )
    ]
    settle(12, pair_in)
    own_half = sums[at(tile * half, half), :]
    for index in range(tiles - 1):
        own_half = own_half + pair_in[index].astype(jnp.float32)
    mid[...] = own_half
    mid_out[...] = own_half.astype(PART_WIRE)
    each(
        shards,
        lambda step: remote(
            mid_out.at[at(lax.rem(shard + step, shards) * chunk, chunk)],
            shard_in.at[step - 1],
            13,
            shard_peer(step),
        ).start(),
    )
    second_acts(2)
    settle(13, shard_in)
    part = lax.fori_loop(
        0,
        shards - 1,
        lambda index, value: value + shard_in[index].astype(jnp.float32),
        mid[at(shard * chunk, chunk), :],
    )
    own = at(tile * half + shard * chunk, chunk)
    total[own, :] = (part * scale).astype(SUM_WIRE)
    each(
        shards,
        lambda step: remote(total.at[own], total.at[own], 14, shard_peer(step)).start(),
    )
    second_acts(3)
    arrive(10)
    arrive(11)
    edge = columns(count * width, width, channels)
    for side, row in ((0, 0), (1, height + 1)):
        rim = spread(flat(rim_in[side]).astype(jnp.float32), edge, width)
        wide[:, row] = rim.reshape(count, width, taps * channels)
    frames(0, count, input_grads)
    stores[2].start()
    if not LATE_OUT:
        all_outputs()
    settle(14, total.at[pl.ds(0, (shards - 1) * chunk)])
    mine = at(tile * half, half)
    each(
        tiles,
        lambda step: remote(total.at[mine], total.at[mine], 15, tile_peer(step)).start(),
    )
    if LATE_OUT:
        all_outputs()
    for index in (0, 1, 6, 7, 8, 9, 10, 11):
        leave(index)
    settle(15, total.at[pl.ds(0, (tiles - 1) * half)])
    split = taps * taps * channels
    grad_s[...] = total[:split, :].astype(jnp.float32)
    stores[3].start()
    grad_t[...] = total[split : split + taps * channels, :].astype(jnp.float32)
    stores[4].start()
    for store in stores:
        store.wait()


def deliver_kernel(*refs):
    count = (len(refs) - 2) // 3
    sources, targets, held = refs[:count], refs[count : 2 * count], refs[2 * count : 3 * count]
    load_sem, store_sem = refs[3 * count :]
    loads, stores = [], []
    for index in range(count):
        loads.append(pltpu.make_async_copy(sources[index], held[index], load_sem.at[index]))
        stores.append(pltpu.make_async_copy(held[index], targets[index], store_sem.at[index]))
    for load in loads:
        load.start()
    for load, store in zip(loads, stores):
        load.wait()
        store.start()
    for store in stores:
        store.wait()


def deliver(*values):
    hbm = pl.BlockSpec(memory_space=pl.ANY)
    count = len(values)
    return pl.pallas_call(
        deliver_kernel,
        out_shape=tuple(jax.ShapeDtypeStruct(value.shape, value.dtype) for value in values),
        in_specs=[hbm] * count,
        out_specs=(hbm,) * count,
        scratch_shapes=[pltpu.VMEM(value.shape, value.dtype) for value in values]
        + [pltpu.SemaphoreType.DMA((count,)), pltpu.SemaphoreType.DMA((count,))],
    )(*values)


def body(latent, cot_forward, cot_reverse, spatial_weight, temporal_weight):
    tiles, shards = lax.axis_size("tile"), lax.axis_size("tm")
    count, height, width, channels = latent.shape
    positions = count * height * width * shards * tiles
    scale = 1.0 / math.sqrt(positions)
    rows = 12 * channels
    unit = 16 * tiles * shards
    padded = -(-rows // unit) * unit
    half = padded // tiles
    chunk = half // shards
    kind = jnp.bfloat16
    vmem = pl.BlockSpec(memory_space=pltpu.VMEM)
    hbm = pl.BlockSpec(memory_space=pl.ANY)
    results = pl.pallas_call(
        functools.partial(kernel, tiles, shards, scale),
        out_shape=(
            jax.ShapeDtypeStruct(latent.shape, kind),
            jax.ShapeDtypeStruct(latent.shape, kind),
            jax.ShapeDtypeStruct(latent.shape, kind),
            jax.ShapeDtypeStruct((9 * channels, channels), jnp.float32),
            jax.ShapeDtypeStruct((3 * channels, channels), jnp.float32),
        ),
        in_specs=[hbm, hbm, hbm, vmem, vmem],
        out_specs=(hbm, hbm, hbm, hbm, hbm),
        scratch_shapes=[
            pltpu.VMEM((count, height + 2, width, channels), kind),
            pltpu.VMEM((count + 2, height, width, channels), kind),
            pltpu.VMEM((count + 2, height, width, channels), kind),
            pltpu.VMEM((count + 4, height, width, channels), kind),
            pltpu.VMEM((count, height * width, channels), jnp.float32),
            pltpu.VMEM((count, height + 2, width, 3 * channels), kind),
            pltpu.VMEM((2, count, width, channels), kind),
            pltpu.VMEM((2, count, width, channels), kind),
            pltpu.VMEM((3 * channels, 3 * channels), kind),
            pltpu.VMEM((channels, 9 * channels), kind),
            pltpu.VMEM((channels, 6 * channels), kind),
            pltpu.VMEM((padded, channels), jnp.float32),
            pltpu.VMEM((padded, channels), PAIR_WIRE),
            pltpu.VMEM((tiles - 1, half, channels), PAIR_WIRE),
            pltpu.VMEM((half, channels), jnp.float32),
            pltpu.VMEM((half, channels), PART_WIRE),
            pltpu.VMEM((shards - 1, chunk, channels), PART_WIRE),
            pltpu.VMEM((padded, channels), SUM_WIRE),
            pltpu.VMEM(latent.shape, kind),
            pltpu.VMEM(latent.shape, kind),
            pltpu.VMEM(latent.shape, kind),
            pltpu.VMEM((9 * channels, channels), jnp.float32),
            pltpu.VMEM((3 * channels, channels), jnp.float32),
            pltpu.SemaphoreType.DMA((3,)),
            pltpu.SemaphoreType.DMA((5,)),
            pltpu.SemaphoreType.DMA((16,)),
            pltpu.SemaphoreType.DMA((16,)),
        ],
        compiler_params=pltpu.CompilerParams(collective_id=0, has_side_effects=True),
    )(
        latent,
        cot_forward,
        cot_reverse,
        spatial_weight.reshape(9 * channels, channels),
        temporal_weight.reshape(3 * channels, channels),
    )
    out_f, out_r, grad_in, grad_s, grad_t = deliver(*results)
    return (
        out_f,
        out_r,
        grad_in,
        grad_s.reshape(spatial_weight.shape),
        grad_t.reshape(temporal_weight.shape),
    )


def solution(mesh):
    placed = (
        P("tm", "tile", None, None),
        P("tm", "tile", None, None),
        P("tm", "tile", None, None),
        P(),
        P(),
    )
    return jax.shard_map(
        body,
        mesh=mesh,
        in_specs=placed,
        out_specs=(
            P("tm", "tile", None, None),
            P("tm", "tile", None, None),
            P("tm", "tile", None, None),
            P(),
            P(),
        ),
        check_vma=False,
    )
```
